256 devices in a mesh: group: 32 (over z, x), member: 4 (over y), pair: 2 (over core).
Axes of the slice: x: 4, y: 4, z: 8, core: 2. Of those that a mesh axis runs over, the one named last changes fastest.
Arguments:
- tokens: bfloat16 [32768, 768], P(('group', 'member', 'pair')), may hold values from -6 to 6
- out_grad: bfloat16 [32768, 768], P(('group', 'member', 'pair')), may hold values from -6 to 6
- router_gate: float32 [32768], P(('group', 'member', 'pair')), may hold values from 0.2 to 1
- expand_weight: bfloat16 [128, 768, 3072], P(('group', 'member'), None, 'pair'), may hold values from -0.21875 to 0.21875
- shrink_weight: bfloat16 [128, 3072, 768], P(('group', 'member'), 'pair'), may hold values from -0.109375 to 0.109375
- expert_ids: int32 [32768], P(('group', 'member', 'pair')), may hold values from 0 to 127, as said below
- slot_ids: int32 [32768], P(('group', 'member', 'pair')), may hold values from 0 to 1, as said below
- capacity: int32 [128], replicated, may hold values from 1 to 2, as said below
Outputs:
- token_grad: bfloat16 [32768, 768], P(('group', 'member', 'pair'))
- expand_grad: bfloat16 [128, 768, 3072], P(('group', 'member'), None, 'pair')
- shrink_grad: bfloat16 [128, 3072, 768], P(('group', 'member'), 'pair')
The draws below stay inside these ranges and needn't reach their ends.
Inputs may be any that keep to these rules, and one draw needn't show every extreme that they name: `expert_ids`: in each aligned block of 128 tokens (the tokens of one device) no expert is named by more than 2 tokens, and one expert, the same for all blocks, is named by exactly 2 tokens in every block. `slot_ids`: A token's slot is the number of earlier tokens of its aligned block of 128 that name the same expert. The expert that is named 2 times in every block has capacity 2.
All inputs are finite; a program needn't handle non-finite values.
Results may differ from the reference program's by a relative error of at most 0.0058.
Values may be sent and summed in bfloat16 or wider, within the bound.
A program may use at most 64 MiB of HBM per device.

```python
import jax
import jax.numpy as jnp
from jax import lax

D = 768
FF = 3072
TOK_DEV = 128
EXPERTS = 128
CAP = 2
TOKENS = 32768


def plan_routes(key):
    base = jax.random.fold_in(key, 11)
    hottest = jax.random.randint(jax.random.fold_in(base, 1), (), 0, EXPERTS)
    blocks = TOKENS // TOK_DEV
    block_keys = jax.random.split(jax.random.fold_in(base, 2), blocks)

    def one_block(block_key):
        first_key, second_key = jax.random.split(block_key)
        cells = jax.random.permutation(first_key, (EXPERTS - 1) * CAP)[:TOK_DEV - CAP]
        others = (hottest + 1 + cells // CAP) % EXPERTS
        chosen = jnp.concatenate([jnp.full((CAP,), hottest, jnp.int32), others.astype(jnp.int32)])
        order = jax.random.permutation(second_key, TOK_DEV)
        chosen = chosen[order]
        onehot = (chosen[:, None] == jnp.arange(EXPERTS, dtype=jnp.int32)[None, :]).astype(jnp.int32)
        earlier = jnp.cumsum(onehot, axis=0) - onehot
        slot = jnp.sum(earlier * onehot, axis=1)
        return (chosen, slot.astype(jnp.int32))
    chosen, slot = jax.vmap(one_block)(block_keys)
    return (chosen.reshape(-1), slot.reshape(-1), hottest)


def draw_expert_ids(key, part):
    return plan_routes(key)[0]


def draw_slot_ids(key, part):
    return plan_routes(key)[1]


def draw_capacity(key, part):
    hottest = plan_routes(key)[2]
    values = jax.random.randint(jax.random.fold_in(key, 23), (EXPERTS,), max(1, CAP // 2), CAP + 1)
    return values.at[hottest].set(CAP).astype(jnp.int32)


def level_of(stream_key, dims, cuts, low, top_value):
    level = 1.0
    for axis_at, shards_of in cuts:
        steps = jax.random.uniform(jax.random.fold_in(jax.random.fold_in(stream_key, 6), axis_at), (shards_of,), jnp.float32, low / len(cuts), top_value / len(cuts))
        level = level * jnp.repeat(jnp.exp(steps), dims[axis_at] // shards_of).reshape((-1,) + (1,) * (len(dims) - 1 - axis_at))
    return level


def gaussian(own_key, dims, spread, bound, shards=(), kind=jnp.bfloat16):
    result = spread * jax.random.normal(own_key, dims, jnp.float32)
    if shards:
        result = result * level_of(own_key, dims, shards, -0.22, 0.18)
    return jnp.clip(result, -bound, bound).astype(kind)


def setup_inputs(seed: int = 0) -> dict:
    seeds = jax.random.split(jax.random.key(seed), 9)
    tokens = gaussian(seeds[0], (TOKENS, D), 1.0, 6.0, ((0, 256),))
    out_grad = gaussian(seeds[1], (TOKENS, D), 1.0, 6.0, ((0, 256),))
    router_gate = jnp.clip(0.2 + 0.8 * jax.random.uniform(seeds[2], (TOKENS,), jnp.float32) ** level_of(seeds[2], (TOKENS,), ((0, 256),), -0.2, 0.2), 0.2, 1.0)
    expand_weight = gaussian(seeds[3], (EXPERTS, D, FF), D ** -0.5, 0.21875, ((0, 128), (2, 2)))
    shrink_weight = gaussian(seeds[4], (EXPERTS, FF, D), FF ** -0.5, 0.109375, ((0, 128), (1, 2)))
    expert_ids = draw_expert_ids(jax.random.fold_in(seeds[8], 71), 0)
    slot_ids = draw_slot_ids(jax.random.fold_in(seeds[8], 71), 0)
    capacity = draw_capacity(jax.random.fold_in(seeds[8], 71), 0)
    return {"tokens": tokens, "out_grad": out_grad, "router_gate": router_gate, "expand_weight": expand_weight, "shrink_weight": shrink_weight, "expert_ids": expert_ids, "slot_ids": slot_ids, "capacity": capacity}


def activation(value):
    return jax.nn.gelu(value, approximate=True)

def expert_pass(operands):
    token_rows, grad_rows, expand_one, shrink_one = operands
    preact = jnp.dot(token_rows, expand_one, preferred_element_type=jnp.float32)
    hidden, pullback = jax.vjp(activation, preact)
    hidden_low = hidden.astype(jnp.bfloat16)
    post_grad = jnp.dot(grad_rows, shrink_one.T, preferred_element_type=jnp.float32)
    pre_grad = pullback(post_grad)[0].astype(jnp.bfloat16)
    expand_part = jnp.dot(token_rows.T, pre_grad, preferred_element_type=jnp.float32).astype(jnp.bfloat16)
    shrink_part = jnp.dot(hidden_low.T, grad_rows, preferred_element_type=jnp.float32).astype(jnp.bfloat16)
    row_grad = jnp.dot(pre_grad, expand_one.T, preferred_element_type=jnp.float32).astype(jnp.bfloat16)
    return (expand_part, shrink_part, row_grad)

def reference(tokens, out_grad, router_gate, expand_weight, shrink_weight, expert_ids, slot_ids, capacity):
    sources = TOKENS // TOK_DEV
    row_count = sources * CAP
    device = (jnp.arange(TOKENS, dtype=jnp.int32) // TOK_DEV).astype(jnp.int32)
    keep_mask = slot_ids < capacity[expert_ids]
    target = jnp.where(keep_mask, expert_ids * row_count + device * CAP + slot_ids, EXPERTS * row_count).astype(jnp.int32)
    scaled = (router_gate[:, None] * out_grad.astype(jnp.float32)).astype(jnp.bfloat16)
    token_buffer = jnp.zeros((EXPERTS * row_count, D), jnp.bfloat16).at[target].set(tokens, mode='drop')
    grad_buffer = jnp.zeros((EXPERTS * row_count, D), jnp.bfloat16).at[target].set(scaled, mode='drop')
    token_buffer = token_buffer.reshape(EXPERTS, row_count, D)
    grad_buffer = grad_buffer.reshape(EXPERTS, row_count, D)
    expand_grad, shrink_grad, row_grad = lax.map(expert_pass, (token_buffer, grad_buffer, expand_weight, shrink_weight))
    flattened = row_grad.reshape(EXPERTS * row_count, D)
    picked = flattened[jnp.minimum(target, EXPERTS * row_count - 1)]
    token_grad = jnp.where(keep_mask[:, None], picked, jnp.zeros((), jnp.bfloat16)).astype(jnp.bfloat16)
    return (token_grad, expand_grad, shrink_grad)
```

```python
import jax
import jax.numpy as jnp
from jax import lax
from jax.sharding import PartitionSpec as P


def activation(value):
    return jax.nn.gelu(value, approximate=True)


def expert_pass(token_rows, grad_rows, expand, shrink):
    f32 = jnp.float32
    preact = jnp.einsum("rd,df->rf", token_rows, expand, preferred_element_type=f32)
    hidden, pullback = jax.vjp(activation, preact)
    hidden_low = hidden.astype(jnp.bfloat16)
    post_grad = jnp.einsum("rd,fd->rf", grad_rows, shrink, preferred_element_type=f32)
    pre_grad = pullback(post_grad)[0].astype(jnp.bfloat16)
    partial_value = jnp.einsum("rf,df->rd", pre_grad, expand, preferred_element_type=f32)
    expand_part = jnp.einsum("rd,rf->df", token_rows, pre_grad, preferred_element_type=f32)
    shrink_part = jnp.einsum("rf,rd->fd", hidden_low, grad_rows, preferred_element_type=f32)
    return expand_part.astype(jnp.bfloat16), shrink_part.astype(jnp.bfloat16), partial_value


def per_device(
    tokens, out_grad, router_gate, expand_weight, shrink_weight, expert_ids, slot_ids, capacity
):
    tok_dev, width = tokens.shape
    experts = capacity.shape[0]
    slots = max(2, 2 * tok_dev // experts)
    f32, bf16 = jnp.float32, jnp.bfloat16
    table = jnp.arange(experts, dtype=jnp.int32)
    limits = jnp.sum(jnp.where(expert_ids[:, None] == table[None, :], capacity[None, :], 0), axis=1)
    keep = slot_ids < limits
    target = jnp.where(keep, expert_ids * slots + slot_ids, experts * slots)
    place = (jnp.arange(experts * slots, dtype=jnp.int32)[:, None] == target[None, :]).astype(bf16)
    scaled = (router_gate[:, None] * out_grad.astype(f32)).astype(bf16)
    token_send = jnp.dot(place, tokens, preferred_element_type=f32).astype(bf16)
    grad_send = jnp.dot(place, scaled, preferred_element_type=f32).astype(bf16)
    token_send = token_send.reshape(experts, slots, width)
    grad_send = grad_send.reshape(experts, slots, width)
    axes = ("group", "member")
    token_rows = lax.all_to_all(token_send, axes, split_axis=0, concat_axis=0, tiled=True)
    grad_rows = lax.all_to_all(grad_send, axes, split_axis=0, concat_axis=0, tiled=True)
    token_rows = lax.all_gather(token_rows.reshape(-1, width), "pair", axis=0, tiled=True)
    grad_rows = lax.all_gather(grad_rows.reshape(-1, width), "pair", axis=0, tiled=True)
    expand_grad, shrink_grad, partial_value = expert_pass(
        token_rows, grad_rows, expand_weight[0], shrink_weight[0]
    )
    rows = experts * slots
    me = lax.axis_index("pair")
    halves = partial_value.reshape(2, rows, width)
    other = lax.ppermute(
        lax.dynamic_index_in_dim(halves, 1 - me, 0, keepdims=False), "pair", ((0, 1), (1, 0))
    )
    summed = lax.dynamic_index_in_dim(halves, me, 0, keepdims=False) + other
    back = summed.astype(bf16).reshape(experts, slots, width)
    back = lax.all_to_all(back, axes, split_axis=0, concat_axis=0, tiled=True)
    token_grad = lax.dot_general(
        place, back.reshape(rows, width), (((0,), (0,)), ((), ())), preferred_element_type=f32
    ).astype(bf16)
    return (token_grad, expand_grad[None], shrink_grad[None])


def solution(mesh):
    placed = (
        P(("group", "member", "pair"), None),
        P(("group", "member", "pair"), None),
        P(("group", "member", "pair")),
        P(("group", "member"), None, "pair"),
        P(("group", "member"), "pair", None),
        P(("group", "member", "pair")),
        P(("group", "member", "pair")),
        P(),
    )
    return jax.shard_map(
        per_device,
        mesh=mesh,
        in_specs=placed,
        out_specs=(
            P(("group", "member", "pair"), None),
            P(("group", "member"), None, "pair"),
            P(("group", "member"), "pair", None),
        ),
        check_vma=False,
    )
```

```python
import functools

import jax
import jax.numpy as jnp
from jax import lax
from jax.experimental import pallas as pl
from jax.experimental.pallas import tpu as pltpu
from jax.sharding import PartitionSpec as P

MESH = pl.DeviceIdType.MESH
F32 = jnp.float32
BF16 = jnp.bfloat16
CHUNKS = 4
HIDDEN_TILE = 256
GELU_C = 0.7978845608028654
GELU_A = 0.044715
NT = (((1,), (1,)), ((), ()))
TN = (((0,), (0,)), ((), ()))


def dot(a, b, dims=(((1,), (0,)), ((), ()))):
    return lax.dot_general(a, b, dims, preferred_element_type=F32)


def kernel(
    sizes,
    tokens_hbm,
    out_grad_hbm,
    gate_hbm,
    expert_ids_hbm,
    slot_ids_hbm,
    capacity_hbm,
    expand_hbm,
    shrink_hbm,
    token_grad,
    expand_grad,
    shrink_grad,
    tokens,
    out_grad,
    gate,
    expert_ids,
    slot_ids,
    capacity,
    expand,
    shrink,
    place,
    send,
    own,
    other,
    token_rows,
    grad_rows,
    hidden,
    pre_grad,
    partial,
    reduced,
    back_send,
    back,
    back_rows,
    load_sem,
    send_sem,
    recv_sem,
    self_sem,
    pair_send_sem,
    pair_recv_sem,
    sum_send_sem,
    sum_recv_sem,
    back_send_sem,
    back_recv_sem,
):
    nz, nx, ny = sizes
    peers = nz * nx * ny
    tok_dev, width = tokens.shape
    half_ff = expand.shape[1]
    per = peers // CHUNKS
    half = 2 * per
    rows = 2 * half
    group, member, pair = (lax.axis_index(a) for a in ("group", "member", "pair"))
    z, x = lax.div(group, nx), lax.rem(group, nx)
    me = group * ny + member

    def shift(i):
        dz = lax.rem(5 * i, nz)
        q = lax.rem(lax.div(i, nz) + 2 * lax.rem(i, nz), nx * ny)
        return dz, lax.div(q, ny), lax.rem(q, ny)

    def ahead(i):
        dz, dx, dy = shift(i)
        return lax.rem(z + dz, nz) * nx + lax.rem(x + dx, nx), lax.rem(member + dy, ny)

    def behind(i):
        dz, dx, dy = shift(i)
        return (
            lax.rem(z + nz - dz, nz) * nx + lax.rem(x + nx - dx, nx),
            lax.rem(member + ny - dy, ny),
        )

    pairs = (
        (expert_ids_hbm, expert_ids),
        (slot_ids_hbm, slot_ids),
        (capacity_hbm, capacity),
        (gate_hbm, gate),
        (tokens_hbm, tokens),
        (out_grad_hbm, out_grad),
        (expand_hbm, expand),
        (shrink_hbm, shrink),
    )
    loads = [pltpu.make_async_copy(a, b, load_sem.at[n]) for n, (a, b) in enumerate(pairs)]
    for copy in loads:
        copy.start()

    barrier = pltpu.get_barrier_semaphore()
    pl.semaphore_signal(
        barrier, inc=1, device_id=(group, member, 1 - pair), device_id_type=MESH
    )

    @pl.loop(1, peers)
    def _(i):
        g, m = behind(i)
        pl.semaphore_signal(barrier, inc=1, device_id=(g, m, pair), device_id_type=MESH)

    for copy in loads[:6]:
        copy.wait()
    ids, slots = expert_ids[...], slot_ids[...]
    square = (tok_dev, tok_dev)
    down, along = lax.broadcasted_iota(jnp.int32, square, 0), lax.broadcasted_iota(
        jnp.int32, square, 1
    )
    named = jnp.where(lax.broadcasted_iota(jnp.int32, (peers, tok_dev), 0) == ids, 1.0, 0.0)
    limits = dot(
        jnp.broadcast_to(capacity[...].astype(F32), (8, peers)).astype(BF16), named.astype(BF16)
    )[0:1, :]
    target = jnp.where(slots.astype(F32) < limits, 2 * ids + slots, 4 * peers)
    place[...] = jnp.where(
        lax.broadcasted_iota(jnp.int32, (2 * peers, tok_dev), 0) == target, 1.0, 0.0
    ).astype(BF16)
    gates = jnp.sum(jnp.where(down == along, gate[...], 0.0), axis=1, keepdims=True)
    scaled = (gates * out_grad[...].astype(F32)).astype(BF16)
    grad_rows[pl.ds(0, tok_dev), :] = scaled

    @pl.loop(0, 8)
    def _(b):
        block = place[pl.ds(pl.multiple_of(b * (peers // 4), peers // 4), peers // 4), :]
        to = pl.ds(b * (peers // 8), peers // 8)
        shape = (peers // 8, 2, width)
        send[to, 0] = dot(block, tokens[...]).astype(BF16).reshape(shape)
        send[to, 1] = dot(block, grad_rows[pl.ds(0, tok_dev), :]).astype(BF16).reshape(shape)

    pl.semaphore_wait(barrier, peers)
    self_copy = pltpu.make_async_copy(send.at[me], own.at[0], self_sem.at[0])
    self_copy.start()

    for c in range(CHUNKS):

        @pl.loop(max(1, c * per), (c + 1) * per)
        def _(i, c=c):
            g, m = ahead(i)
            pltpu.make_async_remote_copy(
                send.at[g * ny + m],
                own.at[i],
                send_sem,
                recv_sem.at[c],
                device_id=(g, m, pair),
                device_id_type=MESH,
            ).start()

    def pair_copy(c):
        part = pl.ds(c * per, per)
        return pltpu.make_async_remote_copy(
            own.at[part],
            other.at[part],
            pair_send_sem.at[c],
            pair_recv_sem.at[c],
            device_id=(group, member, 1 - pair),
            device_id_type=MESH,
        )

    def sum_copy(c):
        return pltpu.make_async_remote_copy(
            partial.at[c, 1],
            reduced.at[c],
            sum_send_sem.at[c],
            sum_recv_sem.at[c],
            device_id=(group, member, 1 - pair),
            device_id_type=MESH,
        )

    def lay_rows(source, c, at):
        step = 16

        @pl.loop(0, per // step)
        def _(b):
            take = pl.ds(c * per + b * step, step)
            to = pl.ds(pl.multiple_of(c * rows + at + b * 2 * step, 2 * step), 2 * step)
            token_rows[to, :] = source[take, 0].reshape(2 * step, width)
            grad_rows[to, :] = source[take, 1].reshape(2 * step, width)

    def chain(c):
        take = pl.ds(c * rows, rows)

        @pl.loop(0, half_ff // HIDDEN_TILE)
        def _(f):
            tile = pl.ds(pl.multiple_of(f * HIDDEN_TILE, HIDDEN_TILE), HIDDEN_TILE)
            v = dot(token_rows[take, :], expand[:, tile])
            post = dot(grad_rows[take, :], shrink[tile, :], NT)
            square_v = v * v
            t = jnp.tanh(GELU_C * (v + GELU_A * (v * square_v)))
            lower = 0.5 * (1.0 + t)
            hidden[take, tile] = (v * lower).astype(BF16)
            slope = lower + (0.5 * v) * (1.0 - t * t) * (
                GELU_C + (3.0 * GELU_A * GELU_C) * square_v
            )
            pre_grad[take, tile] = (slope * post).astype(BF16)

        @pl.loop(0, width // 256)
        def _(d):
            tile = pl.ds(pl.multiple_of(d * 256, 256), 256)
            value = dot(pre_grad[take, :], expand[tile, :], NT)
            partial[c, 0, :, tile] = value[:half]
            partial[c, 1, :, tile] = value[half:]

    def finish(c):
        sum_copy(c).wait_recv()
        step = 16

        @pl.loop(0, per // step)
        def _(b):
            take = pl.ds(pl.multiple_of(b * 2 * step, 2 * step), 2 * step)
            value = (partial[c, 0, take, :] + reduced[c, take, :]).astype(BF16)
            back_send[pl.ds(c * per + b * step, step)] = value.reshape(step, 2, width)

        if c == 0:
            pltpu.make_async_copy(back_send.at[0], back.at[me], self_sem.at[1]).start()

        @pl.loop(max(1, c * per), (c + 1) * per)
        def _(i):
            g, m = behind(i)
            pltpu.make_async_remote_copy(
                back_send.at[i],
                back.at[me],
                back_send_sem,
                back_recv_sem,
                device_id=(g, m, pair),
                device_id_type=MESH,
            ).start()

    for c in range(CHUNKS):
        if c == 0:
            self_copy.wait()
        landed = own.at[pl.ds(max(1, c * per), per - (c == 0))]
        pltpu.make_async_copy(landed, landed, recv_sem.at[c]).wait()
        pair_copy(c).start()
        lay_rows(own, c, 0)
        if c == 0:
            for copy in loads[6:]:
                copy.wait()
        else:
            finish(c - 1)
        pair_copy(c).wait_recv()
        lay_rows(other, c, half)
        chain(c)
        sum_copy(c).start()
    finish(CHUNKS - 1)

    @pl.loop(0, half_ff // 256)
    def _(f):
        tile = pl.ds(pl.multiple_of(f * 256, 256), 256)
        shrink_grad[tile, :] = dot(hidden[:, tile], grad_rows[...], TN).astype(BF16)

        @pl.loop(0, width // 256)
        def _(d):
            part = pl.ds(pl.multiple_of(d * 256, 256), 256)
            expand_grad[part, tile] = dot(token_rows[:, part], pre_grad[:, tile], TN).astype(BF16)

    returned = back.at[pl.ds(0, peers - 1)]
    pltpu.make_async_copy(returned, returned, back_recv_sem).wait()
    pltpu.make_async_copy(back_send.at[0], back.at[me], self_sem.at[1]).wait()

    @pl.loop(0, peers // 16)
    def _(b):
        to = pl.ds(pl.multiple_of(b * 32, 32), 32)
        back_rows[to, :] = back[pl.ds(b * 16, 16)].reshape(32, width)

    token_grad[...] = dot(place[...], back_rows[...], TN).astype(BF16)

    sent = send.at[pl.ds(0, peers - 1)]
    pltpu.make_async_copy(sent, sent, send_sem).wait()
    pltpu.make_async_copy(returned, returned, back_send_sem).wait()
    for c in range(CHUNKS):
        pair_copy(c).wait_send()
        sum_copy(c).wait_send()


def per_device(
    sizes, tokens, out_grad, router_gate, expand_weight, shrink_weight, expert_ids, slot_ids, capacity
):
    tok_dev, width = tokens.shape
    peers = capacity.shape[0]
    half_ff = expand_weight.shape[2]
    per = peers // CHUNKS
    rows = 4 * peers
    vmem = pl.BlockSpec(memory_space=pltpu.VMEM)
    hbm = pl.BlockSpec(memory_space=pltpu.HBM)
    dma = pltpu.SemaphoreType.DMA
    token_grad, expand_grad, shrink_grad = pl.pallas_call(
        functools.partial(kernel, sizes),
        out_shape=(
            pltpu.VMEM((tok_dev, width), BF16),
            pltpu.VMEM((width, half_ff), BF16),
            pltpu.VMEM((half_ff, width), BF16),
        ),
        in_specs=[hbm] * 8,
        out_specs=(vmem, vmem, vmem),
        scratch_shapes=[
            pltpu.VMEM((tok_dev, width), BF16),
            pltpu.VMEM((tok_dev, width), BF16),
            pltpu.VMEM((1, tok_dev), F32),
            pltpu.VMEM((1, tok_dev), jnp.int32),
            pltpu.VMEM((1, tok_dev), jnp.int32),
            pltpu.VMEM((1, peers), jnp.int32),
            pltpu.VMEM((width, half_ff), BF16),
            pltpu.VMEM((half_ff, width), BF16),
            pltpu.VMEM((2 * peers, tok_dev), BF16),
            pltpu.VMEM((peers, 2, 2, width), BF16),
            pltpu.VMEM((peers, 2, 2, width), BF16),
            pltpu.VMEM((peers, 2, 2, width), BF16),
            pltpu.VMEM((rows, width), BF16),
            pltpu.VMEM((rows, width), BF16),
            pltpu.VMEM((rows, half_ff), BF16),
            pltpu.VMEM((rows, half_ff), BF16),
            pltpu.VMEM((CHUNKS, 2, 2 * per, width), F32),
            pltpu.VMEM((CHUNKS, 2 * per, width), F32),
            pltpu.VMEM((peers, 2, width), BF16),
            pltpu.VMEM((peers, 2, width), BF16),
            pltpu.VMEM((2 * peers, width), BF16),
            dma((8,)),
            dma,
            dma((CHUNKS,)),
            dma((2,)),
            dma((CHUNKS,)),
            dma((CHUNKS,)),
            dma((CHUNKS,)),
            dma((CHUNKS,)),
            dma,
            dma,
        ],
        compiler_params=pltpu.CompilerParams(
            collective_id=0, has_side_effects=True, vmem_limit_bytes=44 << 20
        ),
        name="expert_backward",
    )(
        *(
            pltpu.with_memory_space_constraint(a, pltpu.HBM)
            for a in (
                tokens,
                out_grad,
                router_gate.reshape(1, tok_dev),
                expert_ids.reshape(1, tok_dev),
                slot_ids.reshape(1, tok_dev),
                capacity.reshape(1, peers),
                expand_weight.reshape(width, half_ff),
                shrink_weight.reshape(half_ff, width),
            )
        )
    )
    return token_grad, expand_grad[None], shrink_grad[None]


def solution(mesh):
    group, member, _ = (mesh.shape[a] for a in ("group", "member", "pair"))
    nx = 4
    placed = (
        P(("group", "member", "pair"), None),
        P(("group", "member", "pair"), None),
        P(("group", "member", "pair")),
        P(("group", "member"), None, "pair"),
        P(("group", "member"), "pair", None),
        P(("group", "member", "pair")),
        P(("group", "member", "pair")),
        P(),
    )
    return jax.shard_map(
        functools.partial(per_device, (group // nx, nx, member)),
        mesh=mesh,
        in_specs=placed,
        out_specs=(
            P(("group", "member", "pair"), None),
            P(("group", "member"), None, "pair"),
            P(("group", "member"), "pair", None),
        ),
        check_vma=False,
    )
```

```python
import functools

import jax
import jax.numpy as jnp
from jax import lax
from jax.experimental import pallas as pl
from jax.experimental.pallas import tpu as pltpu
from jax.sharding import PartitionSpec as P

MESH = pl.DeviceIdType.MESH
F32 = jnp.float32
BF16 = jnp.bfloat16
PARTS = (32, 32, 32, 32)
HIDDEN_TILE = 256
GELU_C = 0.7978845608028654
GELU_A = 0.044715
NT = (((1,), (1,)), ((), ()))
TN = (((0,), (0,)), ((), ()))


def dot(a, b, dims=(((1,), (0,)), ((), ()))):
    return lax.dot_general(a, b, dims, preferred_element_type=F32)


def kernel(
    sizes,
    tokens_hbm,
    out_grad_hbm,
    gate_hbm,
    expert_ids_hbm,
    slot_ids_hbm,
    capacity_hbm,
    expand_hbm,
    shrink_hbm,
    token_grad,
    expand_grad,
    shrink_grad,
    tokens,
    out_grad,
    gate,
    expert_ids,
    slot_ids,
    capacity,
    expand,
    shrink,
    place,
    send,
    own,
    other,
    token_rows,
    grad_rows,
    hidden,
    pre_grad,
    partial,
    reduced,
    back_send,
    back,
    back_rows,
    load_sem,
    send_sem,
    recv_sem,
    self_sem,
    pair_send_sem,
    pair_recv_sem,
    sum_send_sem,
    sum_recv_sem,
    back_send_sem,
    back_recv_sem,
):
    nz, nx, ny = sizes
    peers = nz * nx * ny
    tok_dev, width = tokens.shape
    half_ff = expand.shape[1]
    first = [sum(PARTS[:c]) for c in range(len(PARTS))]
    group, member, pair = (lax.axis_index(a) for a in ("group", "member", "pair"))
    z, x = lax.div(group, nx), lax.rem(group, nx)
    me = group * ny + member

    def shift(i):
        dz = lax.rem(5 * i, nz)
        q = lax.rem(lax.div(i, nz) + 2 * lax.rem(i, nz), nx * ny)
        return dz, lax.div(q, ny), lax.rem(q, ny)

    def ahead(i):
        dz, dx, dy = shift(i)
        return lax.rem(z + dz, nz) * nx + lax.rem(x + dx, nx), lax.rem(member + dy, ny)

    def behind(i):
        dz, dx, dy = shift(i)
        return (
            lax.rem(z + nz - dz, nz) * nx + lax.rem(x + nx - dx, nx),
            lax.rem(member + ny - dy, ny),
        )

    pairs = (
        (expert_ids_hbm, expert_ids),
        (slot_ids_hbm, slot_ids),
        (capacity_hbm, capacity),
        (gate_hbm, gate),
        (tokens_hbm, tokens),
        (out_grad_hbm, out_grad),
        (expand_hbm, expand),
        (shrink_hbm, shrink),
    )
    loads = [pltpu.make_async_copy(a, b, load_sem.at[n]) for n, (a, b) in enumerate(pairs)]
    for copy in loads:
        copy.start()

    barrier = pltpu.get_barrier_semaphore()
    pl.semaphore_signal(
        barrier, inc=1, device_id=(group, member, 1 - pair), device_id_type=MESH
    )

    @pl.loop(1, peers)
    def _(i):
        g, m = behind(i)
        pl.semaphore_signal(barrier, inc=1, device_id=(g, m, pair), device_id_type=MESH)

    for copy in loads[:6]:
        copy.wait()
    ids, slots = expert_ids[...], slot_ids[...]
    square = (tok_dev, tok_dev)
    down, along = lax.broadcasted_iota(jnp.int32, square, 0), lax.broadcasted_iota(
        jnp.int32, square, 1
    )
    named = jnp.where(lax.broadcasted_iota(jnp.int32, (peers, tok_dev), 0) == ids, 1.0, 0.0)
    limits = dot(
        jnp.broadcast_to(capacity[...].astype(F32), (8, peers)).astype(BF16), named.astype(BF16)
    )[0:1, :]
    target = jnp.where(slots.astype(F32) < limits, 2 * ids + slots, 4 * peers)
    place[...] = jnp.where(
        lax.broadcasted_iota(jnp.int32, (2 * peers, tok_dev), 0) == target, 1.0, 0.0
    ).astype(BF16)
    gates = jnp.sum(jnp.where(down == along, gate[...], 0.0), axis=1, keepdims=True)
    scaled = (gates * out_grad[...].astype(F32)).astype(BF16)
    grad_rows[pl.ds(0, tok_dev), :] = scaled

    @pl.loop(0, 8)
    def _(b):
        block = place[pl.ds(pl.multiple_of(b * (peers // 4), peers // 4), peers // 4), :]
        to = pl.ds(b * (peers // 8), peers // 8)
        shape = (peers // 8, 2, width)
        send[to, 0] = dot(block, tokens[...]).astype(BF16).reshape(shape)
        send[to, 1] = dot(block, grad_rows[pl.ds(0, tok_dev), :]).astype(BF16).reshape(shape)

    pl.semaphore_wait(barrier, peers)
    self_copy = pltpu.make_async_copy(send.at[me], own.at[0], self_sem.at[0])
    self_copy.start()

    for c, at in enumerate(first):

        @pl.loop(max(1, at), at + PARTS[c])
        def _(i, c=c):
            g, m = ahead(i)
            pltpu.make_async_remote_copy(
                send.at[g * ny + m],
                own.at[i],
                send_sem,
                recv_sem.at[c],
                device_id=(g, m, pair),
                device_id_type=MESH,
            ).start()

    def pair_copy(c):
        part = pl.ds(first[c], PARTS[c])
        return pltpu.make_async_remote_copy(
            own.at[part],
            other.at[part],
            pair_send_sem.at[c],
            pair_recv_sem.at[c],
            device_id=(group, member, 1 - pair),
            device_id_type=MESH,
        )

    def sum_copy(c):
        return pltpu.make_async_remote_copy(
            partial.at[1, pl.ds(2 * first[c], 2 * PARTS[c])],
            reduced.at[pl.ds(2 * first[c], 2 * PARTS[c])],
            sum_send_sem.at[c],
            sum_recv_sem.at[c],
            device_id=(group, member, 1 - pair),
            device_id_type=MESH,
        )

    def lay_rows(source, c, at):
        step = 16

        @pl.loop(0, PARTS[c] // step)
        def _(b):
            take = pl.ds(first[c] + b * step, step)
            to = pl.ds(pl.multiple_of(4 * first[c] + at + b * 2 * step, 2 * step), 2 * step)
            token_rows[to, :] = source[take, 0].reshape(2 * step, width)
            grad_rows[to, :] = source[take, 1].reshape(2 * step, width)

    def chain(c):
        half = 2 * PARTS[c]
        take = pl.ds(4 * first[c], 2 * half)
        for f in range(0, half_ff, HIDDEN_TILE):
            tile = pl.ds(f, HIDDEN_TILE)
            v = dot(token_rows[take, :], expand[:, tile])
            post = dot(grad_rows[take, :], shrink[tile, :], NT)
            square_v = v * v
            t = jnp.tanh(v * (GELU_C + (GELU_C * GELU_A) * square_v))
            lower = 0.5 + 0.5 * t
            hidden[take, tile] = (v * lower).astype(BF16)
            slope = lower + v * (1.0 - t * t) * (
                0.5 * GELU_C + (1.5 * GELU_A * GELU_C) * square_v
            )
            pre_grad[take, tile] = (slope * post).astype(BF16)
        for d in range(0, width, 256):
            tile = pl.ds(d, 256)
            value = dot(pre_grad[take, :], expand[tile, :], NT)
            partial[0, pl.ds(2 * first[c], half), tile] = value[:half]
            partial[1, pl.ds(2 * first[c], half), tile] = value[half:]

    def finish(c):
        sum_copy(c).wait_recv()
        step = 16

        @pl.loop(0, PARTS[c] // step)
        def _(b):
            take = pl.ds(pl.multiple_of(2 * first[c] + b * 2 * step, 2 * step), 2 * step)
            value = (partial[0, take, :] + reduced[take, :]).astype(BF16)
            back_send[pl.ds(first[c] + b * step, step)] = value.reshape(step, 2, width)

        if c == 0:
            pltpu.make_async_copy(back_send.at[0], back.at[me], self_sem.at[1]).start()

        @pl.loop(max(1, first[c]), first[c] + PARTS[c])
        def _(i):
            g, m = behind(i)
            pltpu.make_async_remote_copy(
                back_send.at[i],
                back.at[me],
                back_send_sem,
                back_recv_sem,
                device_id=(g, m, pair),
                device_id_type=MESH,
            ).start()

    for c in range(len(PARTS)):
        if c == 0:
            self_copy.wait()
        landed = own.at[pl.ds(max(1, first[c]), PARTS[c] - (c == 0))]
        pltpu.make_async_copy(landed, landed, recv_sem.at[c]).wait()
        pair_copy(c).start()
        lay_rows(own, c, 0)
        if c == 0:
            for copy in loads[6:]:
                copy.wait()
        else:
            finish(c - 1)
        pair_copy(c).wait_recv()
        lay_rows(other, c, 2 * PARTS[c])
        chain(c)
        sum_copy(c).start()
    finish(len(PARTS) - 1)

    @pl.loop(0, half_ff // 256)
    def _(f):
        tile = pl.ds(pl.multiple_of(f * 256, 256), 256)
        shrink_grad[tile, :] = dot(hidden[:, tile], grad_rows[...], TN).astype(BF16)

    @pl.loop(0, width // 256)
    def _(d):
        part = pl.ds(pl.multiple_of(d * 256, 256), 256)
        turned = token_rows[:, part].T
        for f in range(0, half_ff, 256):
            tile = pl.ds(f, 256)
            expand_grad[part, tile] = dot(turned, pre_grad[:, tile]).astype(BF16)

    returned = back.at[pl.ds(0, peers - 1)]
    pltpu.make_async_copy(returned, returned, back_recv_sem).wait()
    pltpu.make_async_copy(back_send.at[0], back.at[me], self_sem.at[1]).wait()

    @pl.loop(0, peers // 16)
    def _(b):
        to = pl.ds(pl.multiple_of(b * 32, 32), 32)
        back_rows[to, :] = back[pl.ds(b * 16, 16)].reshape(32, width)

    token_grad[...] = dot(place[...], back_rows[...], TN).astype(BF16)

    sent = send.at[pl.ds(0, peers - 1)]
    pltpu.make_async_copy(sent, sent, send_sem).wait()
    pltpu.make_async_copy(returned, returned, back_send_sem).wait()
    for c in range(len(PARTS)):
        pair_copy(c).wait_send()
        sum_copy(c).wait_send()


def per_device(
    sizes, tokens, out_grad, router_gate, expand_weight, shrink_weight, expert_ids, slot_ids, capacity
):
    tok_dev, width = tokens.shape
    peers = capacity.shape[0]
    half_ff = expand_weight.shape[2]
    count = len(PARTS)
    rows = 4 * peers
    vmem = pl.BlockSpec(memory_space=pltpu.VMEM)
    hbm = pl.BlockSpec(memory_space=pltpu.HBM)
    dma = pltpu.SemaphoreType.DMA
    token_grad, expand_grad, shrink_grad = pl.pallas_call(
        functools.partial(kernel, sizes),
        out_shape=(
            pltpu.VMEM((tok_dev, width), BF16),
            pltpu.VMEM((width, half_ff), BF16),
            pltpu.VMEM((half_ff, width), BF16),
        ),
        in_specs=[hbm] * 8,
        out_specs=(vmem, vmem, vmem),
        scratch_shapes=[
            pltpu.VMEM((tok_dev, width), BF16),
            pltpu.VMEM((tok_dev, width), BF16),
            pltpu.VMEM((1, tok_dev), F32),
            pltpu.VMEM((1, tok_dev), jnp.int32),
            pltpu.VMEM((1, tok_dev), jnp.int32),
            pltpu.VMEM((1, peers), jnp.int32),
            pltpu.VMEM((width, half_ff), BF16),
            pltpu.VMEM((half_ff, width), BF16),
            pltpu.VMEM((2 * peers, tok_dev), BF16),
            pltpu.VMEM((peers, 2, 2, width), BF16),
            pltpu.VMEM((peers, 2, 2, width), BF16),
            pltpu.VMEM((peers, 2, 2, width), BF16),
            pltpu.VMEM((rows, width), BF16),
            pltpu.VMEM((rows, width), BF16),
            pltpu.VMEM((rows, half_ff), BF16),
            pltpu.VMEM((rows, half_ff), BF16),
            pltpu.VMEM((2, 2 * peers, width), F32),
            pltpu.VMEM((2 * peers, width), F32),
            pltpu.VMEM((peers, 2, width), BF16),
            pltpu.VMEM((peers, 2, width), BF16),
            pltpu.VMEM((2 * peers, width), BF16),
            dma((8,)),
            dma,
            dma((count,)),
            dma((2,)),
            dma((count,)),
            dma((count,)),
            dma((count,)),
            dma((count,)),
            dma,
            dma,
        ],
        compiler_params=pltpu.CompilerParams(
            collective_id=0, has_side_effects=True, vmem_limit_bytes=44 << 20
        ),
        name="expert_backward",
    )(
        *(
            pltpu.with_memory_space_constraint(a, pltpu.HBM)
            for a in (
                tokens,
                out_grad,
                router_gate.reshape(1, tok_dev),
                expert_ids.reshape(1, tok_dev),
                slot_ids.reshape(1, tok_dev),
                capacity.reshape(1, peers),
                expand_weight.reshape(width, half_ff),
                shrink_weight.reshape(half_ff, width),
            )
        )
    )
    return token_grad, expand_grad[None], shrink_grad[None]


def solution(mesh):
    group, member, _ = (mesh.shape[a] for a in ("group", "member", "pair"))
    nx = 4
    placed = (
        P(("group", "member", "pair"), None),
        P(("group", "member", "pair"), None),
        P(("group", "member", "pair")),
        P(("group", "member"), None, "pair"),
        P(("group", "member"), "pair", None),
        P(("group", "member", "pair")),
        P(("group", "member", "pair")),
        P(),
    )
    return jax.shard_map(
        functools.partial(per_device, (group // nx, nx, member)),
        mesh=mesh,
        in_specs=placed,
        out_specs=(
            P(("group", "member", "pair"), None),
            P(("group", "member"), None, "pair"),
            P(("group", "member"), "pair", None),
        ),
        check_vma=False,
    )
```

```python
import functools

import jax
import jax.numpy as jnp
from jax import lax
from jax.experimental import pallas as pl
from jax.experimental.pallas import tpu as pltpu
from jax.sharding import PartitionSpec as P

MESH = pl.DeviceIdType.MESH
F32 = jnp.float32
BF16 = jnp.bfloat16
PARTS = (32, 32, 32, 32)
HIDDEN_TILE = 256
GELU_C = 0.7978845608028654
GELU_A = 0.044715
NT = (((1,), (1,)), ((), ()))
TN = (((0,), (0,)), ((), ()))


def dot(a, b, dims=(((1,), (0,)), ((), ()))):
    return lax.dot_general(a, b, dims, preferred_element_type=F32)


def kernel(
    sizes,
    tokens_hbm,
    out_grad_hbm,
    gate_hbm,
    expert_ids_hbm,
    slot_ids_hbm,
    capacity_hbm,
    expand_hbm,
    shrink_hbm,
    token_grad,
    expand_grad,
    shrink_grad,
    tokens,
    out_grad,
    gate,
    expert_ids,
    slot_ids,
    capacity,
    expand,
    shrink,
    place,
    send,
    own,
    other,
    token_rows,
    grad_rows,
    hidden,
    pre_grad,
    partial,
    reduced,
    back_send,
    back,
    back_rows,
    load_sem,
    send_sem,
    recv_sem,
    self_sem,
    pair_send_sem,
    pair_recv_sem,
    sum_send_sem,
    sum_recv_sem,
    back_send_sem,
    back_recv_sem,
):
    nz, nx, ny = sizes
    peers = nz * nx * ny
    tok_dev, width = tokens.shape
    half_ff = expand.shape[1]
    last = len(PARTS) - 1
    first = [sum(PARTS[:c]) for c in range(len(PARTS))]
    group, member, pair = (lax.axis_index(a) for a in ("group", "member", "pair"))
    z, x = lax.div(group, nx), lax.rem(group, nx)
    me = group * ny + member

    ring = nx * ny
    xs = [[lax.rem(x + n, nx) for n in range(nx)], [lax.rem(x + nx - n, nx) for n in range(nx)]]
    ys = [
        [lax.rem(member + n, ny) for n in range(ny)],
        [lax.rem(member + ny - n, ny) for n in range(ny)],
    ]

    def ahead(j, r):
        zz = lax.rem(z + j + 5 * r % nz, nz)
        return zz * nx + xs[0][r // ny], ys[0][r % ny]

    def behind(j, r):
        zz = lax.rem(z + 2 * nz - j - 5 * r % nz, nz)
        return zz * nx + xs[1][r // ny], ys[1][r % ny]

    def each(start, stop, body):
        @pl.loop(start // ring, stop // ring)
        def _(j):
            for r in range(ring):
                if r or start:
                    body(j, r)
                else:
                    pl.when(j > 0)(functools.partial(body, j, r))

    pairs = (
        (expert_ids_hbm, expert_ids),
        (slot_ids_hbm, slot_ids),
        (capacity_hbm, capacity),
        (gate_hbm, gate),
        (tokens_hbm, tokens),
        (out_grad_hbm, out_grad),
        (expand_hbm, expand),
        (shrink_hbm, shrink),
    )
    loads = [pltpu.make_async_copy(a, b, load_sem.at[n]) for n, (a, b) in enumerate(pairs)]
    for copy in loads:
        copy.start()

    barrier = pltpu.get_barrier_semaphore()
    pl.semaphore_signal(
        barrier, inc=1, device_id=(group, member, 1 - pair), device_id_type=MESH
    )

    def greet(j, r):
        g, m = behind(j, r)
        pl.semaphore_signal(barrier, inc=1, device_id=(g, m, pair), device_id_type=MESH)

    each(0, peers, greet)

    for copy in loads[:6]:
        copy.wait()
    ids, slots = expert_ids[...], slot_ids[...]
    square = (tok_dev, tok_dev)
    down, along = lax.broadcasted_iota(jnp.int32, square, 0), lax.broadcasted_iota(
        jnp.int32, square, 1
    )
    named = jnp.where(lax.broadcasted_iota(jnp.int32, (peers, tok_dev), 0) == ids, 1.0, 0.0)
    limits = dot(
        jnp.broadcast_to(capacity[...].astype(F32), (8, peers)).astype(BF16), named.astype(BF16)
    )[0:1, :]
    target = jnp.where(slots.astype(F32) < limits, 2 * ids + slots, 4 * peers)
    place[...] = jnp.where(
        lax.broadcasted_iota(jnp.int32, (2 * peers, tok_dev), 0) == target, 1.0, 0.0
    ).astype(BF16)
    gates = jnp.sum(jnp.where(down == along, gate[...], 0.0), axis=1, keepdims=True)
    scaled = (gates * out_grad[...].astype(F32)).astype(BF16)
    grad_rows[pl.ds(0, tok_dev), :] = scaled

    @pl.loop(0, 8)
    def _(b):
        block = place[pl.ds(pl.multiple_of(b * (peers // 4), peers // 4), peers // 4), :]
        to = pl.ds(b * (peers // 8), peers // 8)
        shape = (peers // 8, 2, width)
        send[to, 0] = dot(block, tokens[...]).astype(BF16).reshape(shape)
        send[to, 1] = dot(block, grad_rows[pl.ds(0, tok_dev), :]).astype(BF16).reshape(shape)

    pl.semaphore_wait(barrier, peers)
    self_copy = pltpu.make_async_copy(send.at[me], own.at[0], self_sem.at[0])
    self_copy.start()

    for c, at in enumerate(first):

        def give(j, r, c=c):
            g, m = ahead(j, r)
            pltpu.make_async_remote_copy(
                send.at[g * ny + m],
                own.at[ring * j + r],
                send_sem,
                recv_sem.at[c],
                device_id=(g, m, pair),
                device_id_type=MESH,
            ).start()

        each(at, at + PARTS[c], give)

    def pair_copy(c):
        part = pl.ds(first[c], PARTS[c])
        return pltpu.make_async_remote_copy(
            own.at[part],
            other.at[part],
            pair_send_sem.at[c],
            pair_recv_sem.at[c],
            device_id=(group, member, 1 - pair),
            device_id_type=MESH,
        )

    def sum_copy(c):
        return pltpu.make_async_remote_copy(
            partial.at[1, pl.ds(2 * first[c], 2 * PARTS[c])],
            reduced.at[pl.ds(2 * first[c], 2 * PARTS[c])],
            sum_send_sem.at[c],
            sum_recv_sem.at[c],
            device_id=(group, member, 1 - pair),
            device_id_type=MESH,
        )

    def lay_rows(source, c, at):
        step = 16

        @pl.loop(0, PARTS[c] // step)
        def _(b):
            take = pl.ds(first[c] + b * step, step)
            to = pl.ds(pl.multiple_of(4 * first[c] + at + b * 2 * step, 2 * step), 2 * step)
            token_rows[to, :] = source[take, 0].reshape(2 * step, width)
            grad_rows[to, :] = source[take, 1].reshape(2 * step, width)

    def chain(c):
        half = 2 * PARTS[c]
        take = pl.ds(4 * first[c], 2 * half)
        for f in range(0, half_ff, HIDDEN_TILE):
            tile = pl.ds(f, HIDDEN_TILE)
            v = dot(token_rows[take, :], expand[:, tile])
            post = dot(grad_rows[take, :], shrink[tile, :], NT)
            square_v = v * v
            t = jnp.tanh(v * (GELU_C + (GELU_C * GELU_A) * square_v))
            lower = 0.5 + 0.5 * t
            hidden[take, tile] = (v * lower).astype(BF16)
            slope = lower + v * (1.0 - t * t) * (
                0.5 * GELU_C + (1.5 * GELU_A * GELU_C) * square_v
            )
            pre_grad[take, tile] = (slope * post).astype(BF16)
        for d in range(0, width, 256):
            tile = pl.ds(d, 256)
            value = dot(pre_grad[take, :], expand[tile, :], NT)
            partial[0, pl.ds(2 * first[c], half), tile] = value[:half]
            partial[1, pl.ds(2 * first[c], half), tile] = value[half:]

    def finish(c):
        sum_copy(c).wait_recv()
        step = 16

        @pl.loop(0, PARTS[c] // step)
        def _(b):
            take = pl.ds(pl.multiple_of(2 * first[c] + b * 2 * step, 2 * step), 2 * step)
            value = (partial[0, take, :] + reduced[take, :]).astype(BF16)
            back_send[pl.ds(first[c] + b * step, step)] = value.reshape(step, 2, width)

        if c == 0:
            pltpu.make_async_copy(back_send.at[0], back.at[me], self_sem.at[1]).start()

        def give(j, r):
            g, m = behind(j, r)
            pltpu.make_async_remote_copy(
                back_send.at[ring * j + r],
                back.at[me],
                back_send_sem,
                back_recv_sem,
                device_id=(g, m, pair),
                device_id_type=MESH,
            ).start()

        each(first[c], first[c] + PARTS[c], give)

    for c in range(len(PARTS)):
        if c == 0:
            self_copy.wait()
        landed = own.at[pl.ds(max(1, first[c]), PARTS[c] - (c == 0))]
        pltpu.make_async_copy(landed, landed, recv_sem.at[c]).wait()
        pair_copy(c).start()
        lay_rows(own, c, 0)
        if c == 0:
            for copy in loads[6:]:
                copy.wait()
        else:
            finish(c - 1)
        pair_copy(c).wait_recv()
        lay_rows(other, c, 2 * PARTS[c])
        chain(c)
        sum_copy(c).start()
    finish(last)

    @pl.loop(0, half_ff // 256)
    def _(f):
        tile = pl.ds(pl.multiple_of(f * 256, 256), 256)
        shrink_grad[tile, :] = dot(hidden[:, tile], grad_rows[...], TN).astype(BF16)

    @pl.loop(0, width // 256)
    def _(d):
        part = pl.ds(pl.multiple_of(d * 256, 256), 256)
        turned = token_rows[:, part].T
        for f in range(0, half_ff, 256):
            tile = pl.ds(f, 256)
            expand_grad[part, tile] = dot(turned, pre_grad[:, tile]).astype(BF16)

    returned = back.at[pl.ds(0, peers - 1)]
    pltpu.make_async_copy(returned, returned, back_recv_sem).wait()
    pltpu.make_async_copy(back_send.at[0], back.at[me], self_sem.at[1]).wait()

    @pl.loop(0, peers // 16)
    def _(b):
        to = pl.ds(pl.multiple_of(b * 32, 32), 32)
        back_rows[to, :] = back[pl.ds(b * 16, 16)].reshape(32, width)

    token_grad[...] = dot(place[...], back_rows[...], TN).astype(BF16)

    sent = send.at[pl.ds(0, peers - 1)]
    pltpu.make_async_copy(sent, sent, send_sem).wait()
    pltpu.make_async_copy(returned, returned, back_send_sem).wait()
    for c in range(len(PARTS)):
        pair_copy(c).wait_send()
        sum_copy(c).wait_send()


def write(*refs):
    sems = refs[-1]
    copies = [pltpu.make_async_copy(refs[n], refs[3 + n], sems.at[n]) for n in (2, 1, 0)]
    for copy in copies:
        copy.start()
    for copy in copies:
        copy.wait()


def per_device(
    sizes, tokens, out_grad, router_gate, expand_weight, shrink_weight, expert_ids, slot_ids, capacity
):
    tok_dev, width = tokens.shape
    peers = capacity.shape[0]
    half_ff = expand_weight.shape[2]
    count = len(PARTS)
    rows = 4 * peers
    vmem = pl.BlockSpec(memory_space=pltpu.VMEM)
    hbm = pl.BlockSpec(memory_space=pltpu.HBM)
    dma = pltpu.SemaphoreType.DMA
    token_grad, expand_grad, shrink_grad = pl.pallas_call(
        functools.partial(kernel, sizes),
        out_shape=(
            pltpu.VMEM((tok_dev, width), BF16),
            pltpu.VMEM((width, half_ff), BF16),
            pltpu.VMEM((half_ff, width), BF16),
        ),
        in_specs=[hbm] * 8,
        out_specs=(vmem, vmem, vmem),
        scratch_shapes=[
            pltpu.VMEM((tok_dev, width), BF16),
            pltpu.VMEM((tok_dev, width), BF16),
            pltpu.VMEM((1, tok_dev), F32),
            pltpu.VMEM((1, tok_dev), jnp.int32),
            pltpu.VMEM((1, tok_dev), jnp.int32),
            pltpu.VMEM((1, peers), jnp.int32),
            pltpu.VMEM((width, half_ff), BF16),
            pltpu.VMEM((half_ff, width), BF16),
            pltpu.VMEM((2 * peers, tok_dev), BF16),
            pltpu.VMEM((peers, 2, 2, width), BF16),
            pltpu.VMEM((peers, 2, 2, width), BF16),
            pltpu.VMEM((peers, 2, 2, width), BF16),
            pltpu.VMEM((rows, width), BF16),
            pltpu.VMEM((rows, width), BF16),
            pltpu.VMEM((rows, half_ff), BF16),
            pltpu.VMEM((rows, half_ff), BF16),
            pltpu.VMEM((2, 2 * peers, width), F32),
            pltpu.VMEM((2 * peers, width), F32),
            pltpu.VMEM((peers, 2, width), BF16),
            pltpu.VMEM((peers, 2, width), BF16),
            pltpu.VMEM((2 * peers, width), BF16),
            dma((8,)),
            dma,
            dma((count,)),
            dma((2,)),
            dma((count,)),
            dma((count,)),
            dma((count,)),
            dma((count,)),
            dma,
            dma,
        ],
        compiler_params=pltpu.CompilerParams(
            collective_id=0, has_side_effects=True, vmem_limit_bytes=44 << 20
        ),
        name="expert_backward",
    )(
        *(
            pltpu.with_memory_space_constraint(a, pltpu.HBM)
            for a in (
                tokens,
                out_grad,
                router_gate.reshape(1, tok_dev),
                expert_ids.reshape(1, tok_dev),
                slot_ids.reshape(1, tok_dev),
                capacity.reshape(1, peers),
                expand_weight.reshape(width, half_ff),
                shrink_weight.reshape(half_ff, width),
            )
        )
    )
    results = (token_grad, expand_grad, shrink_grad)
    token_grad, expand_grad, shrink_grad = pl.pallas_call(
        write,
        out_shape=tuple(pltpu.HBM(a.shape, a.dtype) for a in results),
        in_specs=[vmem] * 3,
        out_specs=(hbm,) * 3,
        scratch_shapes=[dma((3,))],
        compiler_params=pltpu.CompilerParams(vmem_limit_bytes=16 << 20),
        name="write_results",
    )(*(pltpu.with_memory_space_constraint(a, pltpu.VMEM) for a in results))
    return token_grad, expand_grad[None], shrink_grad[None]


def solution(mesh):
    group, member, _ = (mesh.shape[a] for a in ("group", "member", "pair"))
    nx = 4
    placed = (
        P(("group", "member", "pair"), None),
        P(("group", "member", "pair"), None),
        P(("group", "member", "pair")),
        P(("group", "member"), None, "pair"),
        P(("group", "member"), "pair", None),
        P(("group", "member", "pair")),
        P(("group", "member", "pair")),
        P(),
    )
    return jax.shard_map(
        functools.partial(per_device, (group // nx, nx, member)),
        mesh=mesh,
        in_specs=placed,
        out_specs=(
            P(("group", "member", "pair"), None),
            P(("group", "member"), None, "pair"),
            P(("group", "member"), "pair", None),
        ),
        check_vma=False,
    )
```

```python
import functools

import jax
import jax.numpy as jnp
from jax import lax
from jax.experimental import pallas as pl
from jax.experimental.pallas import tpu as pltpu
from jax.sharding import PartitionSpec as P

MESH = pl.DeviceIdType.MESH
F32 = jnp.float32
BF16 = jnp.bfloat16
PARTS = (32, 32, 32, 32)
HIDDEN_TILE = 256
GELU_C = 0.7978845608028654
GELU_A = 0.044715
NT = (((1,), (1,)), ((), ()))
TN = (((0,), (0,)), ((), ()))


def dot(a, b, dims=(((1,), (0,)), ((), ()))):
    return lax.dot_general(a, b, dims, preferred_element_type=F32)


def kernel(
    sizes,
    tokens_hbm,
    out_grad_hbm,
    gate_hbm,
    expert_ids_hbm,
    slot_ids_hbm,
    capacity_hbm,
    expand_hbm,
    shrink_hbm,
    token_grad,
    expand_grad,
    shrink_grad,
    tokens,
    out_grad,
    gate,
    expert_ids,
    slot_ids,
    capacity,
    expand,
    shrink,
    place,
    send,
    own,
    other,
    token_rows,
    grad_rows,
    hidden,
    pre_grad,
    partial,
    reduced,
    back_send,
    back,
    back_rows,
    load_sem,
    send_sem,
    recv_sem,
    self_sem,
    pair_send_sem,
    pair_recv_sem,
    sum_send_sem,
    sum_recv_sem,
    back_send_sem,
    back_recv_sem,
):
    nz, nx, ny = sizes
    peers = nz * nx * ny
    tok_dev, width = tokens.shape
    half_ff = expand.shape[1]
    last = len(PARTS) - 1
    first = [sum(PARTS[:c]) for c in range(len(PARTS))]
    group, member, pair = (lax.axis_index(a) for a in ("group", "member", "pair"))
    z, x = lax.div(group, nx), lax.rem(group, nx)
    me = group * ny + member

    ring = nx * ny
    xs = [[lax.rem(x + n, nx) for n in range(nx)], [lax.rem(x + nx - n, nx) for n in range(nx)]]
    ys = [
        [lax.rem(member + n, ny) for n in range(ny)],
        [lax.rem(member + ny - n, ny) for n in range(ny)],
    ]

    def ahead(j, r):
        zz = lax.rem(z + j + 5 * r % nz, nz)
        return zz * nx + xs[0][r // ny], ys[0][r % ny]

    def behind(j, r):
        zz = lax.rem(z + 2 * nz - j - 5 * r % nz, nz)
        return zz * nx + xs[1][r // ny], ys[1][r % ny]

    def each(start, stop, body):
        @pl.loop(start // ring, stop // ring)
        def _(j):
            for r in range(ring):
                if r or start:
                    body(j, r)
                else:
                    pl.when(j > 0)(functools.partial(body, j, r))

    pairs = (
        (expert_ids_hbm, expert_ids),
        (slot_ids_hbm, slot_ids),
        (capacity_hbm, capacity),
        (gate_hbm, gate),
        (tokens_hbm, tokens),
        (out_grad_hbm, out_grad),
        (expand_hbm, expand),
        (shrink_hbm, shrink),
    )
    loads = [pltpu.make_async_copy(a, b, load_sem.at[n]) for n, (a, b) in enumerate(pairs)]
    for copy in loads:
        copy.start()

    barrier = pltpu.get_barrier_semaphore()
    pl.semaphore_signal(
        barrier, inc=1, device_id=(group, member, 1 - pair), device_id_type=MESH
    )

    def greet(j, r):
        g, m = behind(j, r)
        pl.semaphore_signal(barrier, inc=1, device_id=(g, m, pair), device_id_type=MESH)

    each(0, peers, greet)

    for copy in loads[:6]:
        copy.wait()
    ids, slots = expert_ids[...], slot_ids[...]
    square = (tok_dev, tok_dev)
    down, along = lax.broadcasted_iota(jnp.int32, square, 0), lax.broadcasted_iota(
        jnp.int32, square, 1
    )
    named = jnp.where(lax.broadcasted_iota(jnp.int32, (peers, tok_dev), 0) == ids, 1.0, 0.0)
    limits = dot(
        jnp.broadcast_to(capacity[...].astype(F32), (8, peers)).astype(BF16), named.astype(BF16)
    )[0:1, :]
    target = jnp.where(slots.astype(F32) < limits, 2 * ids + slots, 4 * peers)
    place[...] = jnp.where(
        lax.broadcasted_iota(jnp.int32, (2 * peers, tok_dev), 0) == target, 1.0, 0.0
    ).astype(BF16)
    gates = jnp.sum(jnp.where(down == along, gate[...], 0.0), axis=1, keepdims=True)
    scaled = (gates * out_grad[...].astype(F32)).astype(BF16)
    grad_rows[pl.ds(0, tok_dev), :] = scaled

    @pl.loop(0, 8)
    def _(b):
        block = place[pl.ds(pl.multiple_of(b * (peers // 4), peers // 4), peers // 4), :]
        to = pl.ds(b * (peers // 8), peers // 8)
        shape = (peers // 8, 2, width)
        send[to, 0] = dot(block, tokens[...]).astype(BF16).reshape(shape)
        send[to, 1] = dot(block, grad_rows[pl.ds(0, tok_dev), :]).astype(BF16).reshape(shape)

    pl.semaphore_wait(barrier, peers)
    self_copy = pltpu.make_async_copy(send.at[me], own.at[0], self_sem.at[0])
    self_copy.start()

    for c, at in enumerate(first):

        def give(j, r, c=c):
            g, m = ahead(j, r)
            pltpu.make_async_remote_copy(
                send.at[g * ny + m],
                own.at[ring * j + r],
                send_sem,
                recv_sem.at[c],
                device_id=(g, m, pair),
                device_id_type=MESH,
            ).start()

        each(at, at + PARTS[c], give)

    def pair_copy(c):
        part = pl.ds(first[c], PARTS[c])
        return pltpu.make_async_remote_copy(
            own.at[part],
            other.at[part],
            pair_send_sem.at[c],
            pair_recv_sem.at[c],
            device_id=(group, member, 1 - pair),
            device_id_type=MESH,
        )

    def sum_copy(c, d):
        part, tile = pl.ds(2 * first[c], 2 * PARTS[c]), pl.ds(256 * d, 256)
        return pltpu.make_async_remote_copy(
            partial.at[1, part, tile],
            reduced.at[part, tile],
            sum_send_sem.at[c, d],
            sum_recv_sem.at[c, d],
            device_id=(group, member, 1 - pair),
            device_id_type=MESH,
        )

    def lay_rows(source, c, at):
        step = 16

        @pl.loop(0, PARTS[c] // step)
        def _(b):
            take = pl.ds(first[c] + b * step, step)
            to = pl.ds(pl.multiple_of(4 * first[c] + at + b * 2 * step, 2 * step), 2 * step)
            token_rows[to, :] = source[take, 0].reshape(2 * step, width)
            grad_rows[to, :] = source[take, 1].reshape(2 * step, width)

    def chain(c):
        half = 2 * PARTS[c]
        take = pl.ds(4 * first[c], 2 * half)
        for f in range(0, half_ff, HIDDEN_TILE):
            tile = pl.ds(f, HIDDEN_TILE)
            v = dot(token_rows[take, :], expand[:, tile])
            post = dot(grad_rows[take, :], shrink[tile, :], NT)
            square_v = v * v
            t = jnp.tanh(v * (GELU_C + (GELU_C * GELU_A) * square_v))
            lower = 0.5 + 0.5 * t
            hidden[take, tile] = (v * lower).astype(BF16)
            slope = lower + v * (1.0 - t * t) * (
                0.5 * GELU_C + (1.5 * GELU_A * GELU_C) * square_v
            )
            pre_grad[take, tile] = (slope * post).astype(BF16)
        for d in range(0, width, 256):
            tile = pl.ds(d, 256)
            value = dot(pre_grad[take, :], expand[tile, :], NT)
            partial[0, pl.ds(2 * first[c], half), tile] = value[:half]
            partial[1, pl.ds(2 * first[c], half), tile] = value[half:]
            sum_copy(c, d // 256).start()

    def finish(c):
        for d in range(width // 256):
            sum_copy(c, d).wait_recv()
        step = 16

        @pl.loop(0, PARTS[c] // step)
        def _(b):
            take = pl.ds(pl.multiple_of(2 * first[c] + b * 2 * step, 2 * step), 2 * step)
            value = (partial[0, take, :] + reduced[take, :]).astype(BF16)
            back_send[pl.ds(first[c] + b * step, step)] = value.reshape(step, 2, width)

        if c == 0:
            pltpu.make_async_copy(back_send.at[0], back.at[me], self_sem.at[1]).start()

        def give(j, r):
            g, m = behind(j, r)
            pltpu.make_async_remote_copy(
                back_send.at[ring * j + r],
                back.at[me],
                back_send_sem,
                back_recv_sem,
                device_id=(g, m, pair),
                device_id_type=MESH,
            ).start()

        each(first[c], first[c] + PARTS[c], give)

    for c in range(len(PARTS)):
        if c == 0:
            self_copy.wait()
        landed = own.at[pl.ds(max(1, first[c]), PARTS[c] - (c == 0))]
        pltpu.make_async_copy(landed, landed, recv_sem.at[c]).wait()
        pair_copy(c).start()
        lay_rows(own, c, 0)
        if c == 0:
            for copy in loads[6:]:
                copy.wait()
        else:
            finish(c - 1)
        pair_copy(c).wait_recv()
        lay_rows(other, c, 2 * PARTS[c])
        chain(c)
    finish(last)

    @pl.loop(0, half_ff // 256)
    def _(f):
        tile = pl.ds(pl.multiple_of(f * 256, 256), 256)
        shrink_grad[tile, :] = dot(hidden[:, tile], grad_rows[...], TN).astype(BF16)

    @pl.loop(0, width // 256)
    def _(d):
        part = pl.ds(pl.multiple_of(d * 256, 256), 256)
        turned = token_rows[:, part].T
        for f in range(0, half_ff, 256):
            tile = pl.ds(f, 256)
            expand_grad[part, tile] = dot(turned, pre_grad[:, tile]).astype(BF16)

    returned = back.at[pl.ds(0, peers - 1)]
    pltpu.make_async_copy(returned, returned, back_recv_sem).wait()
    pltpu.make_async_copy(back_send.at[0], back.at[me], self_sem.at[1]).wait()

    @pl.loop(0, peers // 16)
    def _(b):
        to = pl.ds(pl.multiple_of(b * 32, 32), 32)
        back_rows[to, :] = back[pl.ds(b * 16, 16)].reshape(32, width)

    token_grad[...] = dot(place[...], back_rows[...], TN).astype(BF16)

    sent = send.at[pl.ds(0, peers - 1)]
    pltpu.make_async_copy(sent, sent, send_sem).wait()
    pltpu.make_async_copy(returned, returned, back_send_sem).wait()
    for c in range(len(PARTS)):
        pair_copy(c).wait_send()
        for d in range(width // 256):
            sum_copy(c, d).wait_send()


def write(*refs):
    sems = refs[-1]
    copies = [pltpu.make_async_copy(refs[n], refs[3 + n], sems.at[n]) for n in (2, 1, 0)]
    for copy in copies:
        copy.start()
    for copy in copies:
        copy.wait()


def per_device(
    sizes, tokens, out_grad, router_gate, expand_weight, shrink_weight, expert_ids, slot_ids, capacity
):
    tok_dev, width = tokens.shape
    peers = capacity.shape[0]
    half_ff = expand_weight.shape[2]
    count = len(PARTS)
    rows = 4 * peers
    vmem = pl.BlockSpec(memory_space=pltpu.VMEM)
    hbm = pl.BlockSpec(memory_space=pltpu.HBM)
    dma = pltpu.SemaphoreType.DMA
    token_grad, expand_grad, shrink_grad = pl.pallas_call(
        functools.partial(kernel, sizes),
        out_shape=(
            pltpu.VMEM((tok_dev, width), BF16),
            pltpu.VMEM((width, half_ff), BF16),
            pltpu.VMEM((half_ff, width), BF16),
        ),
        in_specs=[hbm] * 8,
        out_specs=(vmem, vmem, vmem),
        scratch_shapes=[
            pltpu.VMEM((tok_dev, width), BF16),
            pltpu.VMEM((tok_dev, width), BF16),
            pltpu.VMEM((1, tok_dev), F32),
            pltpu.VMEM((1, tok_dev), jnp.int32),
            pltpu.VMEM((1, tok_dev), jnp.int32),
            pltpu.VMEM((1, peers), jnp.int32),
            pltpu.VMEM((width, half_ff), BF16),
            pltpu.VMEM((half_ff, width), BF16),
            pltpu.VMEM((2 * peers, tok_dev), BF16),
            pltpu.VMEM((peers, 2, 2, width), BF16),
            pltpu.VMEM((peers, 2, 2, width), BF16),
            pltpu.VMEM((peers, 2, 2, width), BF16),
            pltpu.VMEM((rows, width), BF16),
            pltpu.VMEM((rows, width), BF16),
            pltpu.VMEM((rows, half_ff), BF16),
            pltpu.VMEM((rows, half_ff), BF16),
            pltpu.VMEM((2, 2 * peers, width), F32),
            pltpu.VMEM((2 * peers, width), F32),
            pltpu.VMEM((peers, 2, width), BF16),
            pltpu.VMEM((peers, 2, width), BF16),
            pltpu.VMEM((2 * peers, width), BF16),
            dma((8,)),
            dma,
            dma((count,)),
            dma((2,)),
            dma((count,)),
            dma((count,)),
            dma((count, width // 256)),
            dma((count, width // 256)),
            dma,
            dma,
        ],
        compiler_params=pltpu.CompilerParams(
            collective_id=0, has_side_effects=True, vmem_limit_bytes=44 << 20
        ),
        name="expert_backward",
    )(
        *(
            pltpu.with_memory_space_constraint(a, pltpu.HBM)
            for a in (
                tokens,
                out_grad,
                router_gate.reshape(1, tok_dev),
                expert_ids.reshape(1, tok_dev),
                slot_ids.reshape(1, tok_dev),
                capacity.reshape(1, peers),
                expand_weight.reshape(width, half_ff),
                shrink_weight.reshape(half_ff, width),
            )
        )
    )
    results = (token_grad, expand_grad, shrink_grad)
    token_grad, expand_grad, shrink_grad = pl.pallas_call(
        write,
        out_shape=tuple(pltpu.HBM(a.shape, a.dtype) for a in results),
        in_specs=[vmem] * 3,
        out_specs=(hbm,) * 3,
        scratch_shapes=[dma((3,))],
        compiler_params=pltpu.CompilerParams(vmem_limit_bytes=16 << 20),
        name="write_results",
    )(*(pltpu.with_memory_space_constraint(a, pltpu.VMEM) for a in results))
    return token_grad, expand_grad[None], shrink_grad[None]


def solution(mesh):
    group, member, _ = (mesh.shape[a] for a in ("group", "member", "pair"))
    nx = 4
    placed = (
        P(("group", "member", "pair"), None),
        P(("group", "member", "pair"), None),
        P(("group", "member", "pair")),
        P(("group", "member"), None, "pair"),
        P(("group", "member"), "pair", None),
        P(("group", "member", "pair")),
        P(("group", "member", "pair")),
        P(),
    )
    return jax.shard_map(
        functools.partial(per_device, (group // nx, nx, member)),
        mesh=mesh,
        in_specs=placed,
        out_specs=(
            P(("group", "member", "pair"), None),
            P(("group", "member"), None, "pair"),
            P(("group", "member"), "pair", None),
        ),
        check_vma=False,
    )
```
